32 devices in a mesh: gx: 8 (over z, x), gy: 4 (over y, core).
Axes of the slice: x: 2, y: 2, z: 4, core: 2. Of those that a mesh axis runs over, the one named last changes fastest.
Arguments:
- object_field: float32 [2, 2048, 1024], P(None, 'gx', 'gy'), may hold values from -4.5 to 4.5
- probe_field: float32 [2, 2, 256, 256], replicated, may hold values from -4.2 to 4.2
- amplitude: float32 [32, 4, 256, 256], P('gx', 'gy'), may hold values from 0.2 to 3
- offsets: int32 [32, 4, 2], P('gx', 'gy'), may hold values from -128 to 128
Outputs:
- updated_object: float32 [2, 2048, 1024], P(None, 'gx', 'gy')
- updated_probe: float32 [2, 2, 256, 256], replicated
The draws below stay inside these ranges and needn't reach their ends.
All inputs are finite; a program needn't handle non-finite values.
Results may differ from the reference program's by a relative error of at most 0.0006.
The reference program's roundings to bfloat16 on the way count: a program that leaves them out, or rounds other values in their place, can miss the bound.
Values sent between devices are 32-bit elements; how exact they have to be, the bound alone decides.
A program may use at most 64 MiB of HBM per device.

```python
import math
import jax
import jax.numpy as jnp
from jax import lax

W = 256
MODES = 2
TILE = 256
POS = 4
NR = 2048
NC = 1024
N_GX = 8
N_GY = 4


def draw_object_field(key, part):
    key_mag = jax.random.fold_in(key, 11)
    key_phase = jax.random.fold_in(key, 12)
    rows = jnp.arange(NR, dtype=jnp.float32)[:, None] / NR
    cols = jnp.arange(NC, dtype=jnp.float32)[None, :] / NC
    ramp = jnp.sqrt((1.0 + 2.0 * rows) * (1.0 + 2.0 * cols)) / 1.7
    rough = jax.random.uniform(key_mag, (NR, NC), jnp.float32, 0.5, 1.2)
    angles = jax.random.uniform(key_phase, (NR, NC), jnp.float32, -math.pi, math.pi)
    magnitude = rough * ramp
    return jnp.stack([magnitude * jnp.cos(angles), magnitude * jnp.sin(angles)], 0)


def touch_ends(entries, key, smallest, high):
    longest = entries.shape.index(max(entries.shape))
    spots = []
    for shift in (0, 1):
        where = [jax.random.randint(jax.random.fold_in(key, axis), (), 0, length) for axis, length in enumerate(entries.shape)]
        where[longest] = (where[longest] + shift) % entries.shape[longest]
        spots.append(tuple(where))
    return entries.at[spots[0]].set(smallest).at[spots[1]].set(high)


def levels(rng, dims, split, smallest, largest):
    level = 1.0
    for axis_at, shards_of in split:
        draws = jax.random.uniform(jax.random.fold_in(jax.random.fold_in(rng, 6), axis_at), (shards_of,), jnp.float32, smallest / len(split), largest / len(split))
        level = level * jnp.repeat(jnp.exp(draws), dims[axis_at] // shards_of).reshape((-1,) + (1,) * (len(dims) - 1 - axis_at))
    return level


def scatter_about(key, dims, scale, most, kind=jnp.bfloat16):
    entries = scale * jax.random.normal(key, dims, jnp.float32)
    return jnp.clip(entries, min=-most, max=most).astype(kind)


def setup_inputs(seed: int = 0) -> dict:
    keys = jax.random.split(jax.random.key(seed), 5)
    object_field = draw_object_field(jax.random.fold_in(keys[4], 71), 0)
    probe_field = scatter_about(keys[1], (MODES, 2, W, W), 0.7, 4.2, jnp.float32)
    amplitude = jnp.clip(jnp.exp(math.log(3.0) - 2.7080502 * jax.random.uniform(keys[2], (POS * N_GX, N_GY, W, W), jnp.float32) ** levels(keys[2], (POS * N_GX, N_GY, W, W), ((0, 8), (1, 4)), -0.2, 0.2)), 0.2, 3.0)
    offsets = touch_ends(jax.random.randint(keys[3], (POS * N_GX, N_GY, 2), 0 - W // 2, TILE - W // 2 + 1), jax.random.fold_in(keys[3], 1), 0 - W // 2, (TILE - W // 2 + 1) - 1).astype(jnp.int32)
    return {"object_field": object_field, "probe_field": probe_field, "amplitude": amplitude, "offsets": offsets}


def dft_tables(extent):
    indices = jnp.arange(extent, dtype=jnp.int32)
    phases = indices[:, None] * indices[None, :] % extent
    angles = phases.astype(jnp.float32) * (2.0 * math.pi / extent)
    norm_factor = 1.0 / math.sqrt(extent)
    return ((jnp.cos(angles) * norm_factor).astype(jnp.bfloat16), (jnp.sin(angles) * norm_factor).astype(jnp.bfloat16))

def to_half(values):
    return lax.optimization_barrier(values.astype(jnp.bfloat16)).astype(jnp.float32)

def row_pass(cosine, sine, real_part, imag_part, orient):
    amount = real_part.shape[0]
    stacked = jnp.concatenate([real_part, imag_part], 0).astype(jnp.float32)
    with_cos = jnp.einsum('jk,bkl->bjl', cosine.astype(jnp.float32), stacked)
    with_sin = jnp.einsum('jk,bkl->bjl', sine.astype(jnp.float32), stacked)
    return (with_cos[:amount] + orient * with_sin[amount:], with_cos[amount:] - orient * with_sin[:amount])

def col_pass(cosine, sine, real_part, imag_part, orient):
    amount = real_part.shape[0]
    stacked = jnp.concatenate([real_part, imag_part], 0).astype(jnp.float32)
    with_cos = jnp.einsum('bjk,kl->bjl', stacked, cosine.astype(jnp.float32))
    with_sin = jnp.einsum('bjk,kl->bjl', stacked, sine.astype(jnp.float32))
    return (with_cos[:amount] + orient * with_sin[amount:], with_cos[amount:] - orient * with_sin[:amount])

def corrections(windows, probe_field, amplitude, cosine, sine):
    extent = probe_field.shape[-1]
    obj_real = windows[:, None, 0]
    obj_imag = windows[:, None, 1]
    probe_real = probe_field[None, :, 0]
    probe_imag = probe_field[None, :, 1]
    psi_real = probe_real * obj_real - probe_imag * obj_imag
    psi_imag = probe_real * obj_imag + probe_imag * obj_real
    amount = psi_real.shape[0]
    mode_count = psi_real.shape[1]
    shape_flat = (amount * mode_count, extent, extent)
    shape_full = (amount, mode_count, extent, extent)
    rows_real, rows_imag = row_pass(cosine, sine, to_half(psi_real.reshape(shape_flat)), to_half(psi_imag.reshape(shape_flat)), 1.0)
    far_real, far_imag = col_pass(cosine, sine, to_half(rows_real), to_half(rows_imag), 1.0)
    far_real = far_real.reshape(shape_full)
    far_imag = far_imag.reshape(shape_full)
    intensity = lax.optimization_barrier(jnp.sum(far_real * far_real + far_imag * far_imag, axis=1))
    factor = (amplitude / jnp.maximum(jnp.sqrt(intensity), 0.25))[:, None]
    proj_real = to_half((far_real * factor).reshape(shape_flat))
    proj_imag = to_half((far_imag * factor).reshape(shape_flat))
    back_rows_real, back_rows_imag = row_pass(cosine, sine, proj_real, proj_imag, -1.0)
    back_real, back_imag = col_pass(cosine, sine, to_half(back_rows_real), to_half(back_rows_imag), -1.0)
    diff_real = back_real.reshape(shape_full) - psi_real
    diff_imag = back_imag.reshape(shape_full) - psi_imag
    object_real = lax.optimization_barrier(jnp.sum(probe_real * diff_real + probe_imag * diff_imag, axis=1))
    object_imag = lax.optimization_barrier(jnp.sum(probe_real * diff_imag - probe_imag * diff_real, axis=1))
    grad_real = lax.optimization_barrier(jnp.sum(obj_real * diff_real + obj_imag * diff_imag, axis=0))
    grad_imag = lax.optimization_barrier(jnp.sum(obj_real * diff_imag - obj_imag * diff_real, axis=0))
    weight = lax.optimization_barrier(jnp.sum(windows[:, 0] * windows[:, 0] + windows[:, 1] * windows[:, 1], axis=0))
    return (jnp.stack([object_real, object_imag], 1), grad_real, grad_imag, weight)

def reference(object_field, probe_field, amplitude, offsets):
    extent = probe_field.shape[-1]
    margin = extent // 2
    mode_count = probe_field.shape[0]
    cosine, sine = dft_tables(extent)
    padded = jnp.pad(object_field, ((0, 0), (margin, margin), (margin, margin)), mode='wrap')
    zero_index = jnp.zeros((), jnp.int32)

    def tile_step(running, tile_number):
        accum, grad_real, grad_imag, weight = running
        tile_row = tile_number // N_GY
        tile_col = tile_number % N_GY
        tile_offsets = lax.dynamic_slice(offsets, (tile_row * POS, tile_col, zero_index), (POS, 1, 2))[:, 0]
        tile_amp = lax.dynamic_slice(amplitude, (tile_row * POS, tile_col, zero_index, zero_index), (POS, 1, extent, extent))[:, 0]
        row_starts = (tile_row * TILE + tile_offsets[:, 0] + margin).astype(jnp.int32)
        col_starts = (tile_col * TILE + tile_offsets[:, 1] + margin).astype(jnp.int32)
        windows = jnp.stack([lax.dynamic_slice(padded, (zero_index, row_starts[position], col_starts[position]), (2, extent, extent)) for position in range(POS)], 0)
        terms, step_real, step_imag, step_weight = corrections(windows, probe_field, tile_amp, cosine, sine)
        for position in range(POS):
            where = (zero_index, row_starts[position], col_starts[position])
            current = lax.dynamic_slice(accum, where, (2, extent, extent))
            accum = lax.dynamic_update_slice(accum, current + terms[position], where)
        return ((accum, grad_real + step_real, grad_imag + step_imag, weight + step_weight), None)
    start_state = (jnp.zeros((2, NR + 2 * margin, NC + 2 * margin), jnp.float32), jnp.zeros((mode_count, extent, extent), jnp.float32), jnp.zeros((mode_count, extent, extent), jnp.float32), jnp.zeros((extent, extent), jnp.float32))
    final_state, _ = lax.scan(tile_step, start_state, jnp.arange(N_GX * N_GY, dtype=jnp.int32))
    accum, grad_real, grad_imag, weight = final_state
    cols_core = accum[:, :, margin:margin + NC]
    cols_core = cols_core.at[:, :, NC - margin:].add(accum[:, :, :margin])
    cols_core = cols_core.at[:, :, :margin].add(accum[:, :, NC + margin:])
    object_step = cols_core[:, margin:margin + NR]
    object_step = object_step.at[:, NR - margin:].add(cols_core[:, :margin])
    object_step = object_step.at[:, :margin].add(cols_core[:, NR + margin:])
    updated_probe = probe_field + jnp.stack([grad_real, grad_imag], 1) / (weight + 1e-05)
    power = lax.optimization_barrier(jnp.sum(probe_field * probe_field, axis=(0, 1)))
    scale_max = jnp.max(power) + 1e-06
    updated_object = object_field + object_step / scale_max
    return (updated_object, updated_probe)
```

```python
import functools
import math

import jax
import jax.numpy as jnp
from jax import lax
from jax.experimental import pallas as pl
from jax.experimental.pallas import tpu as pltpu
from jax.sharding import PartitionSpec as P

MESH = pl.DeviceIdType.MESH
VMEM = pl.BlockSpec(memory_space=pltpu.VMEM)
ANY = pl.BlockSpec(memory_space=pl.ANY)
F32 = jnp.float32
BF16 = jnp.bfloat16
CHUNK = 32
SUB = 8


def dft_tables(extent):
    indices = jnp.arange(extent, dtype=jnp.int32)
    phases = indices[:, None] * indices[None, :] % extent
    angles = phases.astype(F32) * (2.0 * math.pi / extent)
    norm_factor = 1.0 / math.sqrt(extent)
    return (
        (jnp.cos(angles) * norm_factor).astype(BF16),
        (jnp.sin(angles) * norm_factor).astype(BF16),
    )


def remote(src, dst, sems, slot, device):
    return pltpu.make_async_remote_copy(
        src_ref=src,
        dst_ref=dst,
        send_sem=sems.at[0, slot],
        recv_sem=sems.at[1, slot],
        device_id=device,
        device_id_type=MESH,
    )


def greet(devices):
    barrier = pltpu.get_barrier_semaphore()
    for device in devices:
        pl.semaphore_signal(barrier, inc=1, device_id=device, device_id_type=MESH)
    pl.semaphore_wait(barrier, len(devices))


def halo_kernel(n_gx, n_gy, margin, obj, ext, sems, local_sem):
    gx, gy = lax.axis_index("gx"), lax.axis_index("gy")
    rows, cols = obj.shape[1], obj.shape[2]
    m = margin
    up = (lax.rem(gx + n_gx - 1, n_gx), gy)
    down = (lax.rem(gx + 1, n_gx), gy)
    left = (gx, lax.rem(gy + n_gy - 1, n_gy))
    right = (gx, lax.rem(gy + 1, n_gy))
    own = pltpu.make_async_copy(
        obj, ext.at[:, pl.ds(m, rows), pl.ds(m, cols)], local_sem.at[0]
    )
    own.start()
    greet((up, down, left, right))
    top, bottom = pl.ds(0, m), pl.ds(m + rows, m)
    lcol, rcol = pl.ds(0, m), pl.ds(m + cols, m)
    mid_r, mid_c = pl.ds(m, rows), pl.ds(m, cols)
    to_down = remote(obj.at[:, pl.ds(rows - m, m), :], ext.at[:, top, mid_c], sems, 0, down)
    to_up = remote(obj.at[:, pl.ds(0, m), :], ext.at[:, bottom, mid_c], sems, 1, up)
    to_right = remote(obj.at[:, :, pl.ds(cols - m, m)], ext.at[:, mid_r, lcol], sems, 2, right)
    to_left = remote(obj.at[:, :, pl.ds(0, m)], ext.at[:, mid_r, rcol], sems, 3, left)
    first = (to_down, to_up, to_right, to_left)
    for copy in first:
        copy.start()
    corners = []
    for copy, band, slot in ((to_down, top, 4), (to_up, bottom, 6)):
        copy.wait_recv()
        a = remote(ext.at[:, band, pl.ds(cols, m)], ext.at[:, band, lcol], sems, slot, right)
        b = remote(ext.at[:, band, pl.ds(m, m)], ext.at[:, band, rcol], sems, slot + 1, left)
        a.start()
        b.start()
        corners += [a, b]
    to_right.wait_recv()
    to_left.wait_recv()
    for copy in corners:
        copy.wait_recv()
    for copy in first:
        copy.wait_send()
    for copy in corners:
        copy.wait_send()
    own.wait()


def update_kernel(
    margin, offs, ext, probe, amp, fr, frt, acc, sums, win, psi, xbuf, ybuf, far
):
    p = pl.program_id(0)
    extent = probe.shape[-1]
    modes = probe.shape[0]
    width = ext.shape[2]
    r0 = offs[p, 0] + margin
    c0 = offs[p, 1] + margin
    back_shift = lax.rem(width - c0, width)
    low = lax.rem(r0, SUB)
    base = r0 - low
    tall = CHUNK + SUB
    row_shift = lax.rem(tall - low, tall)
    n_chunks = extent // CHUNK

    @pl.when(p == 0)
    def _():
        acc[...] = jnp.zeros_like(acc)
        sums[...] = jnp.zeros_like(sums)

    @pl.loop(0, n_chunks)
    def _(i):
        rb = pl.multiple_of(i * CHUNK, CHUNK)
        here = pl.ds(rb, CHUNK)
        w = []
        for part in range(2):
            line = ext[part, pl.ds(pl.multiple_of(base + rb, SUB), tall), :]
            line = pltpu.roll(line, row_shift, 0)[:CHUNK]
            w.append(pltpu.roll(line, back_shift, 1)[:, :extent])
            win[part, here, :] = w[part]
        sums[2 * modes, here, :] += w[0] * w[0] + w[1] * w[1]
        for k in range(modes):
            cols = slice(k * extent, (k + 1) * extent)
            pr, pi = probe[k, 0, here, :], probe[k, 1, here, :]
            psi_re = pr * w[0] - pi * w[1]
            psi_im = pr * w[1] + pi * w[0]
            psi[k, 0, here, :] = psi_re
            psi[k, 1, here, :] = psi_im
            xbuf[here, cols] = psi_re.astype(BF16)
            xbuf[pl.ds(extent + rb, CHUNK), cols] = psi_im.astype(BF16)

    def rows_then_cols(row_table, col_table):
        for part in range(2):
            table = row_table[part * extent : (part + 1) * extent, :]
            out = jnp.dot(table, xbuf[...], preferred_element_type=F32).astype(BF16)
            for k in range(modes):
                ybuf[k * extent : (k + 1) * extent, part * extent : (part + 1) * extent] = out[
                    :, k * extent : (k + 1) * extent
                ]
        for k in range(modes):
            band = slice(k * extent, (k + 1) * extent)
            far[band, :] = jnp.dot(ybuf[band, :], col_table[...], preferred_element_type=F32)

    rows_then_cols(fr, frt)

    @pl.loop(0, n_chunks)
    def _(i):
        rb = pl.multiple_of(i * CHUNK, CHUNK)
        parts = []
        intensity = jnp.zeros((CHUNK, extent), F32)
        for k in range(modes):
            at = pl.ds(k * extent + rb, CHUNK)
            re, im = far[at, :extent], far[at, extent:]
            intensity += re * re + im * im
            parts.append((re, im))
        factor = amp[0, pl.ds(rb, CHUNK), :] * jnp.minimum(lax.rsqrt(intensity), 4.0)
        for k in range(modes):
            cols = slice(k * extent, (k + 1) * extent)
            xbuf[pl.ds(rb, CHUNK), cols] = (parts[k][0] * factor).astype(BF16)
            xbuf[pl.ds(extent + rb, CHUNK), cols] = (parts[k][1] * factor).astype(BF16)

    rows_then_cols(frt, fr)

    @pl.loop(0, n_chunks)
    def _(i):
        rb = pl.multiple_of(i * CHUNK, CHUNK)
        here = pl.ds(rb, CHUNK)
        wr, wi = win[0, here, :], win[1, here, :]
        obj_re = jnp.zeros((CHUNK, extent), F32)
        obj_im = jnp.zeros((CHUNK, extent), F32)
        for k in range(modes):
            at = pl.ds(k * extent + rb, CHUNK)
            dr = far[at, :extent] - psi[k, 0, here, :]
            di = far[at, extent:] - psi[k, 1, here, :]
            pr, pi = probe[k, 0, here, :], probe[k, 1, here, :]
            obj_re += pr * dr + pi * di
            obj_im += pr * di - pi * dr
            sums[2 * k, here, :] += wr * dr + wi * di
            sums[2 * k + 1, here, :] += wr * di - wi * dr
        blank = jnp.zeros((CHUNK, width - extent), F32)
        below = jnp.zeros((SUB, width), F32)
        for part, value in enumerate((obj_re, obj_im)):
            line = pltpu.roll(jnp.concatenate([value, blank], 1), lax.rem(c0, width), 1)
            line = pltpu.roll(jnp.concatenate([line, below], 0), low, 0)
            acc[part, pl.ds(pl.multiple_of(base + rb, SUB), tall), :] += line


def reduce_plan(n_gx, n_gy, rows):
    x_bits = [("gx", b) for b in range(n_gx.bit_length() - 1)]
    y_bits = [("gy", b) for b in range(n_gy.bit_length() - 1)]
    lane_a = y_bits[:1] + x_bits[:1] + y_bits[1:] + x_bits[1:]
    lane_b = y_bits[:1] + y_bits[1:2] + x_bits[:1] + x_bits[1:][::-1] + y_bits[2:]
    return (lane_a, lane_b)


def fold_kernel(n_gx, n_gy, margin, acc, obj, probe, sums, out_obj, out_probe, *scratch):
    (from_left, from_right, send_up, send_down, from_up, from_down, part, inbox, sems) = scratch
    gx, gy = lax.axis_index("gx"), lax.axis_index("gy")
    rows, cols = obj.shape[1], obj.shape[2]
    planes, extent = sums.shape[0], sums.shape[1]
    m = margin
    up = (lax.rem(gx + n_gx - 1, n_gx), gy)
    down = (lax.rem(gx + 1, n_gx), gy)
    left = (gx, lax.rem(gy + n_gy - 1, n_gy))
    right = (gx, lax.rem(gy + 1, n_gy))
    plan = reduce_plan(n_gx, n_gy, extent)

    def partner(axis, bit):
        step = 1 << bit
        coord = gx if axis == "gx" else gy
        mine = lax.rem(coord // step, 2)
        other = coord + step * (1 - 2 * mine)
        return mine, ((other, gy) if axis == "gx" else (gx, other))

    partners = [partner(*b)[1] for b in plan[0]]
    greet([up, down, left, right] + partners)

    slot = [0]

    def send(src, dst, device):
        copy = remote(src, dst, sems, slot[0], device)
        slot[0] += 1
        copy.start()
        return copy

    lcol, rcol = pl.ds(0, m), pl.ds(m + cols, m)
    bands = (pl.ds(0, m), pl.ds(m + rows, m))
    mid = pl.ds(m, rows)

    def strip(band):
        return (
            send(acc.at[:, band, lcol], from_right.at[:, band, :], left),
            send(acc.at[:, band, rcol], from_left.at[:, band, :], right),
        )

    corner = [strip(band) for band in bands]

    lanes = len(plan)
    lane_w = extent // lanes
    state = []
    for lane in range(lanes):
        state.append({"off": 0, "n": extent, "src": sums, "box": 0})
    history = [[] for _ in range(lanes)]
    pending = []

    def start_step(step):
        copies = []
        for lane in range(lanes):
            s = state[lane]
            mine, device = partner(*plan[lane][step])
            at = pl.ds(lane * lane_w, lane_w)
            n = s["n"]
            if n % 16 == 0:
                half = n // 2
                give = pl.ds(pl.multiple_of(s["off"] + (1 - mine) * half, 8), half)
                keep = s["off"] + mine * half
                s["n"] = half
                history[lane].append((device, step))
            else:
                half = n
                give = pl.ds(pl.multiple_of(s["off"], 8), half)
                keep = s["off"]
            box = inbox.at[:, pl.ds(s["box"], half), at]
            s["box"] += half
            s["keep"] = keep
            copies.append((send(s["src"].at[:, give, at], box, device), box, half))
        return copies

    def end_step(copies, dst_index):
        for lane, (copy, box, half) in enumerate(copies):
            s = state[lane]
            at = pl.ds(lane * lane_w, lane_w)
            copy.wait_recv()
            keep = pl.ds(pl.multiple_of(s["keep"], 8), half)
            total = s["src"][:, keep, at] + box[...]
            part[dst_index, :, keep, at] = total
            s["off"] = s["keep"]
        for lane in range(lanes):
            state[lane]["src"] = part.at[dst_index]
        for copy, _, _ in copies:
            pending.append(copy)

    steps = len(plan[0])
    copies = start_step(0)
    end_step(copies, 0)
    copies = start_step(1)

    vertical = []
    middle = None
    for index, (band, buf, box, device) in enumerate(
        ((bands[0], send_up, from_down, up), (bands[1], send_down, from_up, down))
    ):
        for copy in corner[index]:
            copy.wait_recv()
        buf[:, :, :m] = acc[:, band, pl.ds(m, m)] + from_left[:, band, :]
        if cols > 2 * m:
            buf[:, :, m : cols - m] = acc[:, band, pl.ds(2 * m, cols - 2 * m)]
        buf[:, :, cols - m :] = acc[:, band, pl.ds(cols, m)] + from_right[:, band, :]
        vertical.append(send(buf, box, device))
    middle = strip(mid)

    end_step(copies, 1)
    for step in range(2, steps):
        copies = start_step(step)
        end_step(copies, step)

    modes = probe.shape[0]
    for lane in range(lanes):
        s = state[lane]
        at = pl.ds(lane * lane_w, lane_w)
        keep = pl.ds(pl.multiple_of(s["off"], 8), s["n"])
        weight = s["src"][planes - 1, keep, at] + 1e-05
        for k in range(modes):
            for c in range(2):
                out_probe[2 * k + c, keep, at] = (
                    probe[k, c, keep, at] + s["src"][2 * k + c, keep, at] / weight
                )

    def gather_start(level):
        copies = []
        for lane in range(lanes):
            s = state[lane]
            device, step = history[lane][level]
            at = pl.ds(lane * lane_w, lane_w)
            own = pl.ds(pl.multiple_of(s["off"], 8), s["n"])
            copies.append(send(out_probe.at[:, own, at], out_probe.at[:, own, at], device))
        return copies

    def gather_end(level, copies):
        for lane, copy in enumerate(copies):
            s = state[lane]
            _, step = history[lane][level]
            mine, _ = partner(*plan[lane][step])
            s["off"] = s["off"] - mine * s["n"]
            s["n"] = 2 * s["n"]
            copy.wait_recv()
            pending.append(copy)

    levels = len(history[0])
    copies = gather_start(levels - 1)

    power = jnp.zeros((extent, extent), F32)
    for k in range(modes):
        for c in range(2):
            power += probe[k, c] * probe[k, c]
    scale = jnp.max(power, keepdims=True) + 1e-06
    for copy in vertical:
        copy.wait_recv()
    for copy in middle:
        copy.wait_recv()
    for c in range(2):
        step_sum = acc[c, pl.ds(m, rows), pl.ds(m, cols)]
        gap_r = [jnp.zeros((rows - 2 * m, cols), F32)] if rows > 2 * m else []
        gap_c = [jnp.zeros((rows, cols - 2 * m), F32)] if cols > 2 * m else []
        side = jnp.concatenate(
            [from_left[c, pl.ds(m, rows), :]] + gap_c + [from_right[c, pl.ds(m, rows), :]], 1
        )
        ends = jnp.concatenate([from_up[c]] + gap_r + [from_down[c]], 0)
        out_obj[c] = obj[c] + (step_sum + side + ends) / scale

    gather_end(levels - 1, copies)
    for level in range(levels - 2, -1, -1):
        copies = gather_start(level)
        gather_end(level, copies)
    for pair in corner:
        pending.extend(pair)
    pending.extend(vertical)
    pending.extend(middle)
    for copy in pending:
        copy.wait_send()


def body(n_gx, n_gy, object_field, probe_field, amplitude, offsets):
    extent = probe_field.shape[-1]
    modes = probe_field.shape[0]
    margin = extent // 2
    rows, cols = object_field.shape[1:]
    positions = amplitude.shape[0]
    ext_shape = (2, rows + 2 * margin + SUB, cols + 2 * margin)
    ext = pl.pallas_call(
        functools.partial(halo_kernel, n_gx, n_gy, margin),
        out_shape=jax.ShapeDtypeStruct(ext_shape, F32),
        in_specs=[ANY],
        out_specs=VMEM,
        scratch_shapes=[pltpu.SemaphoreType.DMA((2, 8)), pltpu.SemaphoreType.DMA((1,))],
        compiler_params=pltpu.CompilerParams(collective_id=0, has_side_effects=True),
        name="halo",
    )(object_field)

    cosine, sine = dft_tables(extent)
    fr = jnp.concatenate(
        [jnp.concatenate([cosine, sine], 1), jnp.concatenate([-sine, cosine], 1)], 0
    )
    frt = jnp.concatenate(
        [jnp.concatenate([cosine, -sine], 1), jnp.concatenate([sine, cosine], 1)], 0
    )
    planes = 2 * modes + 1
    acc, sums = pl.pallas_call(
        functools.partial(update_kernel, margin),
        grid=(positions,),
        out_shape=(
            jax.ShapeDtypeStruct(ext_shape, F32),
            jax.ShapeDtypeStruct((planes, extent, extent), F32),
        ),
        in_specs=[
            pl.BlockSpec(memory_space=pltpu.SMEM),
            VMEM,
            VMEM,
            pl.BlockSpec((1, extent, extent), lambda i: (i, 0, 0)),
            VMEM,
            VMEM,
        ],
        out_specs=(VMEM, VMEM),
        scratch_shapes=[
            pltpu.VMEM((2, extent, extent), F32),
            pltpu.VMEM((modes, 2, extent, extent), F32),
            pltpu.VMEM((2 * extent, modes * extent), BF16),
            pltpu.VMEM((modes * extent, 2 * extent), BF16),
            pltpu.VMEM((modes * extent, 2 * extent), F32),
        ],
        name="update",
    )(offsets[:, 0, :], ext, probe_field, amplitude[:, 0], fr, frt)

    steps = n_gx.bit_length() + n_gy.bit_length() - 2
    out_obj, out_probe = pl.pallas_call(
        functools.partial(fold_kernel, n_gx, n_gy, margin),
        out_shape=(
            jax.ShapeDtypeStruct(object_field.shape, F32),
            jax.ShapeDtypeStruct((2 * modes, extent, extent), F32),
        ),
        in_specs=[VMEM] * 4,
        out_specs=(VMEM, VMEM),
        scratch_shapes=[
            pltpu.VMEM((2, rows + 2 * margin, margin), F32),
            pltpu.VMEM((2, rows + 2 * margin, margin), F32),
            pltpu.VMEM((2, margin, cols), F32),
            pltpu.VMEM((2, margin, cols), F32),
            pltpu.VMEM((2, margin, cols), F32),
            pltpu.VMEM((2, margin, cols), F32),
            pltpu.VMEM((steps, planes, extent, extent), F32),
            pltpu.VMEM((planes, 2 * extent, extent), F32),
            pltpu.SemaphoreType.DMA((2, 10 + 4 * steps)),
        ],
        compiler_params=pltpu.CompilerParams(collective_id=1, has_side_effects=True),
        name="fold",
    )(acc, object_field, probe_field, sums)
    return out_obj, out_probe.reshape(probe_field.shape)


def solution(mesh):
    in_specs = (P(None, "gx", "gy"), P(), P("gx", "gy", None, None), P("gx", "gy", None))
    out_specs = (P(None, "gx", "gy"), P())
    step = functools.partial(body, mesh.shape["gx"], mesh.shape["gy"])
    return jax.shard_map(step, mesh=mesh, in_specs=in_specs, out_specs=out_specs, check_vma=False)
```

```python
import functools
import math

import jax
import jax.numpy as jnp
import numpy as np
from jax import lax
from jax.experimental import pallas as pl
from jax.experimental.pallas import tpu as pltpu
from jax.sharding import PartitionSpec as P

MESH = pl.DeviceIdType.MESH
VMEM = pl.BlockSpec(memory_space=pltpu.VMEM)
ANY = pl.BlockSpec(memory_space=pl.ANY)
F32 = jnp.float32
BF16 = jnp.bfloat16
CHUNK = 32
SUB = 8
STRIPS = 4


def dft_tables(extent):
    indices = np.arange(extent)
    angles = (indices[:, None] * indices[None, :] % extent) * (2.0 * math.pi / extent)
    norm_factor = 1.0 / math.sqrt(extent)
    both = np.concatenate([np.cos(angles), np.sin(angles)], 1) * norm_factor
    return jnp.asarray(both.astype(np.float32).astype(jnp.bfloat16))


def remote(src, dst, sems, slot, device):
    return pltpu.make_async_remote_copy(
        src_ref=src,
        dst_ref=dst,
        send_sem=sems.at[0, slot],
        recv_sem=sems.at[1, slot],
        device_id=device,
        device_id_type=MESH,
    )


def greet(devices):
    barrier = pltpu.get_barrier_semaphore()
    for device in devices:
        pl.semaphore_signal(barrier, inc=1, device_id=device, device_id_type=MESH)
    pl.semaphore_wait(barrier, len(devices))


def halo_kernel(n_gx, n_gy, margin, obj, ext, sems, local_sem):
    gx, gy = lax.axis_index("gx"), lax.axis_index("gy")
    rows, cols = obj.shape[1], obj.shape[2]
    m = margin
    up = (lax.rem(gx + n_gx - 1, n_gx), gy)
    down = (lax.rem(gx + 1, n_gx), gy)
    left = (gx, lax.rem(gy + n_gy - 1, n_gy))
    right = (gx, lax.rem(gy + 1, n_gy))
    own = pltpu.make_async_copy(
        obj, ext.at[:, pl.ds(m, rows), pl.ds(m, cols)], local_sem.at[0]
    )
    own.start()
    greet((up, down, left, right))
    lcol, rcol = pl.ds(0, m), pl.ds(m + cols, m)
    mid_r, mid_c = pl.ds(m, rows), pl.ds(m, cols)
    piece = m // STRIPS
    slot = [0]

    def send(src, dst, device):
        copy = remote(src, dst, sems, slot[0], device)
        slot[0] += 1
        copy.start()
        return copy

    vertical = []
    for i in range(STRIPS):
        at = i * piece
        for src, dst, device in ((rows - m + at, at, down), (at, m + rows + at, up)):
            band = pl.ds(dst, piece)
            copy = send(obj.at[:, pl.ds(src, piece), :], ext.at[:, band, mid_c], device)
            vertical.append((copy, band))
    pending = [
        send(obj.at[:, :, pl.ds(cols - m, m)], ext.at[:, mid_r, lcol], right),
        send(obj.at[:, :, pl.ds(0, m)], ext.at[:, mid_r, rcol], left),
    ]
    for copy, band in vertical:
        copy.wait_recv()
        pending.append(send(ext.at[:, band, pl.ds(cols, m)], ext.at[:, band, lcol], right))
        pending.append(send(ext.at[:, band, pl.ds(m, m)], ext.at[:, band, rcol], left))
    for copy in pending:
        copy.wait_recv()
    for copy in pending:
        copy.wait_send()
    for copy, _ in vertical:
        copy.wait_send()
    own.wait()


def update_kernel(
    margin, offs, ext, probe, amp, table, acc, sums, win, psi, xbuf, ybuf, far, fr, frt
):
    p = pl.program_id(0)
    extent = probe.shape[-1]
    modes = probe.shape[0]
    width = ext.shape[2]
    r0 = offs[p, 0, 0] + margin
    c0 = offs[p, 0, 1] + margin
    back_shift = lax.rem(width - c0, width)
    low = lax.rem(r0, SUB)
    base = r0 - low
    tall = CHUNK + SUB
    row_shift = lax.rem(tall - low, tall)
    n_chunks = extent // CHUNK

    @pl.when(p == 0)
    def _():
        acc[...] = jnp.zeros_like(acc)
        sums[...] = jnp.zeros_like(sums)
        c, s = table[:, :extent], table[:, extent:]
        fr[:extent, :extent] = c
        fr[:extent, extent:] = s
        fr[extent:, :extent] = -s
        fr[extent:, extent:] = c
        frt[:extent, :extent] = c
        frt[:extent, extent:] = -s
        frt[extent:, :extent] = s
        frt[extent:, extent:] = c

    @pl.loop(0, n_chunks, unroll=2)
    def _(i):
        rb = pl.multiple_of(i * CHUNK, CHUNK)
        here = pl.ds(rb, CHUNK)
        w = []
        for part in range(2):
            line = ext[part, pl.ds(pl.multiple_of(base + rb, SUB), tall), :]
            line = pltpu.roll(line, row_shift, 0)[:CHUNK]
            w.append(pltpu.roll(line, back_shift, 1)[:, :extent])
            win[part, here, :] = w[part]
        sums[2 * modes, here, :] += w[0] * w[0] + w[1] * w[1]
        for k in range(modes):
            cols = slice(k * extent, (k + 1) * extent)
            pr, pi = probe[k, 0, here, :], probe[k, 1, here, :]
            psi_re = pr * w[0] - pi * w[1]
            psi_im = pr * w[1] + pi * w[0]
            psi[k, 0, here, :] = psi_re
            psi[k, 1, here, :] = psi_im
            xbuf[here, cols] = psi_re.astype(BF16)
            xbuf[pl.ds(extent + rb, CHUNK), cols] = psi_im.astype(BF16)

    def rows_then_cols(row_table, col_table):
        for part in range(2):
            table = row_table[part * extent : (part + 1) * extent, :]
            out = jnp.dot(table, xbuf[...], preferred_element_type=F32).astype(BF16)
            for k in range(modes):
                ybuf[k * extent : (k + 1) * extent, part * extent : (part + 1) * extent] = out[
                    :, k * extent : (k + 1) * extent
                ]
        for k in range(modes):
            band = slice(k * extent, (k + 1) * extent)
            far[band, :] = jnp.dot(ybuf[band, :], col_table[...], preferred_element_type=F32)

    rows_then_cols(fr, frt)

    @pl.loop(0, n_chunks, unroll=2)
    def _(i):
        rb = pl.multiple_of(i * CHUNK, CHUNK)
        parts = []
        intensity = jnp.zeros((CHUNK, extent), F32)
        for k in range(modes):
            at = pl.ds(k * extent + rb, CHUNK)
            re, im = far[at, :extent], far[at, extent:]
            intensity += re * re + im * im
            parts.append((re, im))
        factor = amp[0, pl.ds(rb, CHUNK), :] * jnp.minimum(lax.rsqrt(intensity), 4.0)
        for k in range(modes):
            cols = slice(k * extent, (k + 1) * extent)
            xbuf[pl.ds(rb, CHUNK), cols] = (parts[k][0] * factor).astype(BF16)
            xbuf[pl.ds(extent + rb, CHUNK), cols] = (parts[k][1] * factor).astype(BF16)

    rows_then_cols(frt, fr)

    @pl.loop(0, n_chunks, unroll=2)
    def _(i):
        rb = pl.multiple_of(i * CHUNK, CHUNK)
        here = pl.ds(rb, CHUNK)
        wr, wi = win[0, here, :], win[1, here, :]
        obj_re = jnp.zeros((CHUNK, extent), F32)
        obj_im = jnp.zeros((CHUNK, extent), F32)
        for k in range(modes):
            at = pl.ds(k * extent + rb, CHUNK)
            dr = far[at, :extent] - psi[k, 0, here, :]
            di = far[at, extent:] - psi[k, 1, here, :]
            pr, pi = probe[k, 0, here, :], probe[k, 1, here, :]
            obj_re += pr * dr + pi * di
            obj_im += pr * di - pi * dr
            sums[2 * k, here, :] += wr * dr + wi * di
            sums[2 * k + 1, here, :] += wr * di - wi * dr
        blank = jnp.zeros((CHUNK, width - extent), F32)
        below = jnp.zeros((SUB, width), F32)
        for part, value in enumerate((obj_re, obj_im)):
            line = pltpu.roll(jnp.concatenate([value, blank], 1), lax.rem(c0, width), 1)
            line = pltpu.roll(jnp.concatenate([line, below], 0), low, 0)
            acc[part, pl.ds(pl.multiple_of(base + rb, SUB), tall), :] += line


def reduce_plan(n_gx, n_gy):
    x_bits, y_bits = n_gx.bit_length() - 1, n_gy.bit_length() - 1
    core, x, y = ("gy", 0, 1), ("gx", 0, 1), ("gy", 1, 1)
    z = ("gx", 1, min(2, x_bits - 1))
    rest = [("gx", b, 1) for b in range(3, x_bits)] + [("gy", b, 1) for b in range(2, y_bits)]
    return ([core, x, y, z] + rest, [core, y, x, z] + rest)


def fold_kernel(n_gx, n_gy, margin, acc, obj, probe, sums, out_obj, out_probe, *scratch):
    (from_left, from_right, send_up, send_down, from_up, from_down, part, inbox, sems) = scratch
    gx, gy = lax.axis_index("gx"), lax.axis_index("gy")
    rows, cols = obj.shape[1], obj.shape[2]
    planes, extent = sums.shape[0], sums.shape[1]
    modes = probe.shape[0]
    m = margin
    up = (lax.rem(gx + n_gx - 1, n_gx), gy)
    down = (lax.rem(gx + 1, n_gx), gy)
    left = (gx, lax.rem(gy + n_gy - 1, n_gy))
    right = (gx, lax.rem(gy + 1, n_gy))
    plan = reduce_plan(n_gx, n_gy)

    def members(axis, bit, count):
        size, step = 1 << count, 1 << bit
        coord = gx if axis == "gx" else gy
        mine = lax.rem(coord // step, size)
        peers = []
        for d in range(1, size):
            field = lax.rem(mine + d, size)
            other = coord + step * (field - mine)
            peers.append((field, (other, gy) if axis == "gx" else (gx, other)))
        return size, mine, peers

    greet([up, down, left, right] + [dev for g in plan[0] for _, dev in members(*g)[2]])

    slot = [0]
    pending = []

    def send(src, dst, device):
        copy = remote(src, dst, sems, slot[0], device)
        slot[0] += 1
        copy.start()
        pending.append(copy)
        return copy

    lcol, rcol = pl.ds(0, m), pl.ds(m + cols, m)
    bands = (pl.ds(0, m), pl.ds(m + rows, m))
    mid = pl.ds(m, rows)

    def strip(band):
        return (
            send(acc.at[:, band, lcol], from_right.at[:, band, :], left),
            send(acc.at[:, band, rcol], from_left.at[:, band, :], right),
        )

    lanes = len(plan)
    lane_w = extent // lanes
    state = [{"off": 0, "n": extent, "src": sums, "box": 0} for _ in range(lanes)]
    history = [[] for _ in range(lanes)]

    def reduce_start(step):
        started = []
        for lane in range(lanes):
            s = state[lane]
            size, mine, peers = members(*plan[lane][step])
            at = pl.ds(lane * lane_w, lane_w)
            split = s["n"] % (size * SUB) == 0
            n = s["n"] // size if split else s["n"]
            copies = []
            for field, device in peers:
                give = s["off"] + field * n if split else s["off"]
                src = s["src"].at[:, pl.ds(pl.multiple_of(give, SUB), n), at]
                box = inbox.at[:, pl.ds(pl.multiple_of(s["box"] + mine * n, SUB), n), at]
                copies.append(send(src, box, device))
            keep = s["off"] + mine * n if split else s["off"]
            history[lane].append((size, mine, peers, split))
            started.append((copies, keep, n, size, mine, s["box"]))
            s["box"] += size * n
        return started

    def reduce_end(step, started):
        for lane, (copies, keep, n, size, mine, box) in enumerate(started):
            s = state[lane]
            at = pl.ds(lane * lane_w, lane_w)
            own = s["src"][:, pl.ds(pl.multiple_of(keep, SUB), n), at]
            inbox[:, pl.ds(pl.multiple_of(box + mine * n, SUB), n), at] = own
            for copy in copies:
                copy.wait_recv()
            total = inbox[:, pl.ds(box, n), at]
            for j in range(1, size):
                total += inbox[:, pl.ds(box + j * n, n), at]
            part[step, :, pl.ds(pl.multiple_of(keep, SUB), n), at] = total
            s["off"], s["n"], s["src"] = keep, n, part.at[step]

    started = reduce_start(0)
    corner = [strip(band) for band in bands]
    reduce_end(0, started)
    started = reduce_start(1)

    for index, (band, buf) in enumerate(((bands[0], send_up), (bands[1], send_down))):
        for copy in corner[index]:
            copy.wait_recv()
        buf[:, :, :m] = acc[:, band, pl.ds(m, m)] + from_left[:, band, :]
        if cols > 2 * m:
            buf[:, :, m : cols - m] = acc[:, band, pl.ds(2 * m, cols - 2 * m)]
        buf[:, :, cols - m :] = acc[:, band, pl.ds(cols, m)] + from_right[:, band, :]

    def vertical(c):
        return (
            send(send_up.at[c], from_down.at[c], up),
            send(send_down.at[c], from_up.at[c], down),
        )

    reduce_end(1, started)
    started = reduce_start(2)
    folded = vertical(0)
    reduce_end(2, started)
    steps = len(plan[0])
    started = reduce_start(3)
    folded += vertical(1)
    folded += strip(mid)
    reduce_end(3, started)
    for step in range(4, steps):
        started = reduce_start(step)
        reduce_end(step, started)

    for lane in range(lanes):
        s = state[lane]
        at = pl.ds(lane * lane_w, lane_w)
        keep = pl.ds(pl.multiple_of(s["off"], SUB), s["n"])
        weight = s["src"][planes - 1, keep, at] + 1e-05
        for k in range(2 * modes):
            out_probe[k, keep, at] = s["src"][k, keep, at] / weight

    def gather_start(level):
        started = []
        for lane in range(lanes):
            s = state[lane]
            size, mine, peers, split = history[lane][level]
            at = pl.ds(lane * lane_w, lane_w)
            if split:
                own = out_probe.at[:, pl.ds(pl.multiple_of(s["off"], SUB), s["n"]), at]
                started += [send(own, own, device) for _, device in peers]
                s["off"] = s["off"] - mine * s["n"]
                s["n"] *= size
        return started

    def gather_end(started):
        for copy in started:
            copy.wait_recv()

    started = gather_start(steps - 1)
    power = jnp.zeros((extent, extent), F32)
    for k in range(modes):
        for c in range(2):
            power += probe[k, c] * probe[k, c]
    scale = jnp.max(power, keepdims=True) + 1e-06
    for level in range(steps - 2, 0, -1):
        gather_end(started)
        started = gather_start(level)
    for copy in folded:
        copy.wait_recv()
    for c in range(2):
        step_sum = acc[c, pl.ds(m, rows), pl.ds(m, cols)]
        gap_r = [jnp.zeros((rows - 2 * m, cols), F32)] if rows > 2 * m else []
        gap_c = [jnp.zeros((rows, cols - 2 * m), F32)] if cols > 2 * m else []
        side = jnp.concatenate(
            [from_left[c, pl.ds(m, rows), :]] + gap_c + [from_right[c, pl.ds(m, rows), :]], 1
        )
        ends = jnp.concatenate([from_up[c]] + gap_r + [from_down[c]], 0)
        out_obj[c] = (step_sum + side + ends) / scale
    gather_end(started)
    started = gather_start(0)
    gather_end(started)
    for copy in pending:
        copy.wait_send()


def body(n_gx, n_gy, object_field, probe_field, amplitude, offsets):
    extent = probe_field.shape[-1]
    modes = probe_field.shape[0]
    margin = extent // 2
    rows, cols = object_field.shape[1:]
    positions = amplitude.shape[0]
    ext_shape = (2, rows + 2 * margin + SUB, cols + 2 * margin)
    ext = pl.pallas_call(
        functools.partial(halo_kernel, n_gx, n_gy, margin),
        out_shape=jax.ShapeDtypeStruct(ext_shape, F32),
        in_specs=[ANY],
        out_specs=VMEM,
        scratch_shapes=[pltpu.SemaphoreType.DMA((2, 2 + 6 * STRIPS)), pltpu.SemaphoreType.DMA((1,))],
        compiler_params=pltpu.CompilerParams(collective_id=0, has_side_effects=True),
        name="halo",
    )(object_field)

    planes = 2 * modes + 1
    acc, sums = pl.pallas_call(
        functools.partial(update_kernel, margin),
        grid=(positions,),
        out_shape=(
            jax.ShapeDtypeStruct(ext_shape, F32),
            jax.ShapeDtypeStruct((planes, extent, extent), F32),
        ),
        in_specs=[
            pl.BlockSpec(memory_space=pltpu.SMEM),
            VMEM,
            VMEM,
            pl.BlockSpec((1, extent, extent), lambda i: (i, 0, 0)),
            VMEM,
        ],
        out_specs=(VMEM, VMEM),
        scratch_shapes=[
            pltpu.VMEM((2, extent, extent), F32),
            pltpu.VMEM((modes, 2, extent, extent), F32),
            pltpu.VMEM((2 * extent, modes * extent), BF16),
            pltpu.VMEM((modes * extent, 2 * extent), BF16),
            pltpu.VMEM((modes * extent, 2 * extent), F32),
            pltpu.VMEM((2 * extent, 2 * extent), BF16),
            pltpu.VMEM((2 * extent, 2 * extent), BF16),
        ],
        name="update",
    )(offsets, ext, probe_field, amplitude[:, 0], dft_tables(extent))

    plan = reduce_plan(n_gx, n_gy)[0]
    steps = len(plan)
    peers = sum((1 << count) - 1 for _, _, count in plan)
    out_obj, out_probe = pl.pallas_call(
        functools.partial(fold_kernel, n_gx, n_gy, margin),
        out_shape=(
            jax.ShapeDtypeStruct(object_field.shape, F32),
            jax.ShapeDtypeStruct((2 * modes, extent, extent), F32),
        ),
        in_specs=[VMEM] * 4,
        out_specs=(VMEM, VMEM),
        scratch_shapes=[
            pltpu.VMEM((2, rows + 2 * margin, margin), F32),
            pltpu.VMEM((2, rows + 2 * margin, margin), F32),
            pltpu.VMEM((2, margin, cols), F32),
            pltpu.VMEM((2, margin, cols), F32),
            pltpu.VMEM((2, margin, cols), F32),
            pltpu.VMEM((2, margin, cols), F32),
            pltpu.VMEM((steps, planes, extent, extent), F32),
            pltpu.VMEM((planes, 3 * extent, extent), F32),
            pltpu.SemaphoreType.DMA((2, 10 + 4 * peers)),
        ],
        compiler_params=pltpu.CompilerParams(collective_id=1, has_side_effects=True),
        name="fold",
    )(acc, object_field, probe_field, sums)
    return object_field + out_obj, probe_field + out_probe.reshape(probe_field.shape)


def solution(mesh):
    in_specs = (P(None, "gx", "gy"), P(), P("gx", "gy", None, None), P("gx", "gy", None))
    out_specs = (P(None, "gx", "gy"), P())
    step = functools.partial(body, mesh.shape["gx"], mesh.shape["gy"])
    return jax.shard_map(step, mesh=mesh, in_specs=in_specs, out_specs=out_specs, check_vma=False)
```

```python
import functools
import math

import jax
import jax.numpy as jnp
import numpy as np
from jax import lax
from jax.experimental import pallas as pl
from jax.experimental.pallas import tpu as pltpu
from jax.sharding import PartitionSpec as P

MESH = pl.DeviceIdType.MESH
VMEM = pl.BlockSpec(memory_space=pltpu.VMEM)
ANY = pl.BlockSpec(memory_space=pl.ANY)
F32 = jnp.float32
BF16 = jnp.bfloat16
CHUNK = 32
SUB = 8
STRIPS = 4
PIECES = 8
MIDS = 4


def dft_tables(extent):
    indices = np.arange(extent)
    angles = (indices[:, None] * indices[None, :] % extent) * (2.0 * math.pi / extent)
    norm_factor = 1.0 / math.sqrt(extent)
    both = np.concatenate([np.cos(angles), np.sin(angles)], 1) * norm_factor
    return jnp.asarray(both.astype(np.float32).astype(jnp.bfloat16))


def remote(src, dst, sems, slot, device):
    return pltpu.make_async_remote_copy(
        src_ref=src,
        dst_ref=dst,
        send_sem=sems.at[0, slot],
        recv_sem=sems.at[1, slot],
        device_id=device,
        device_id_type=MESH,
    )


def greet(devices):
    barrier = pltpu.get_barrier_semaphore()
    for device in devices:
        pl.semaphore_signal(barrier, inc=1, device_id=device, device_id_type=MESH)
    pl.semaphore_wait(barrier, len(devices))


def halo_kernel(n_gx, n_gy, margin, obj, ext, sems, local_sem):
    gx, gy = lax.axis_index("gx"), lax.axis_index("gy")
    rows, cols = obj.shape[1], obj.shape[2]
    m = margin
    up = (lax.rem(gx + n_gx - 1, n_gx), gy)
    down = (lax.rem(gx + 1, n_gx), gy)
    left = (gx, lax.rem(gy + n_gy - 1, n_gy))
    right = (gx, lax.rem(gy + 1, n_gy))
    own = pltpu.make_async_copy(
        obj, ext.at[:, pl.ds(m, rows), pl.ds(m, cols)], local_sem.at[0]
    )
    own.start()
    greet((up, down, left, right))
    lcol, rcol = pl.ds(0, m), pl.ds(m + cols, m)
    mid_r, mid_c = pl.ds(m, rows), pl.ds(m, cols)
    piece = m // STRIPS
    slot = [0]

    def send(src, dst, device):
        copy = remote(src, dst, sems, slot[0], device)
        slot[0] += 1
        copy.start()
        return copy

    vertical = []
    for i in range(STRIPS):
        at = i * piece
        for src, dst, device in ((rows - m + at, at, down), (at, m + rows + at, up)):
            band = pl.ds(dst, piece)
            copy = send(obj.at[:, pl.ds(src, piece), :], ext.at[:, band, mid_c], device)
            vertical.append((copy, band))
    pending = [
        send(obj.at[:, :, pl.ds(cols - m, m)], ext.at[:, mid_r, lcol], right),
        send(obj.at[:, :, pl.ds(0, m)], ext.at[:, mid_r, rcol], left),
    ]
    for copy, band in vertical:
        copy.wait_recv()
        pending.append(send(ext.at[:, band, pl.ds(cols, m)], ext.at[:, band, lcol], right))
        pending.append(send(ext.at[:, band, pl.ds(m, m)], ext.at[:, band, rcol], left))
    for copy in pending:
        copy.wait_recv()
    for copy in pending:
        copy.wait_send()
    for copy, _ in vertical:
        copy.wait_send()
    own.wait()


def update_kernel(
    margin, offs, ext, probe, amp, table, acc, sums, win, psi, xbuf, ybuf, far, fr, frt
):
    p = pl.program_id(0)
    extent = probe.shape[-1]
    modes = probe.shape[0]
    width = ext.shape[2]
    r0 = offs[p, 0, 0] + margin
    c0 = offs[p, 0, 1] + margin
    back_shift = lax.rem(width - c0, width)
    low = lax.rem(r0, SUB)
    base = r0 - low
    tall = CHUNK + SUB
    row_shift = lax.rem(tall - low, tall)
    n_chunks = extent // CHUNK

    @pl.when(p == 0)
    def _():
        acc[...] = jnp.zeros_like(acc)
        sums[...] = jnp.zeros_like(sums)
        c, s = table[:, :extent], table[:, extent:]
        fr[:extent, :extent] = c
        fr[:extent, extent:] = s
        fr[extent:, :extent] = -s
        fr[extent:, extent:] = c
        frt[:extent, :extent] = c
        frt[:extent, extent:] = -s
        frt[extent:, :extent] = s
        frt[extent:, extent:] = c

    @pl.loop(0, n_chunks, unroll=4)
    def _(i):
        rb = pl.multiple_of(i * CHUNK, CHUNK)
        here = pl.ds(rb, CHUNK)
        w = []
        for part in range(2):
            line = ext[part, pl.ds(pl.multiple_of(base + rb, SUB), tall), :]
            line = pltpu.roll(line, row_shift, 0)[:CHUNK]
            w.append(pltpu.roll(line, back_shift, 1)[:, :extent])
            win[part, here, :] = w[part]
        sums[2 * modes, here, :] += w[0] * w[0] + w[1] * w[1]
        for k in range(modes):
            cols = slice(k * extent, (k + 1) * extent)
            pr, pi = probe[k, 0, here, :], probe[k, 1, here, :]
            psi_re = pr * w[0] - pi * w[1]
            psi_im = pr * w[1] + pi * w[0]
            psi[k, 0, here, :] = psi_re
            psi[k, 1, here, :] = psi_im
            xbuf[here, cols] = psi_re.astype(BF16)
            xbuf[pl.ds(extent + rb, CHUNK), cols] = psi_im.astype(BF16)

    def rows_then_cols(row_table, col_table):
        for part in range(2):
            table = row_table[part * extent : (part + 1) * extent, :]
            out = jnp.dot(table, xbuf[...], preferred_element_type=F32).astype(BF16)
            for k in range(modes):
                ybuf[k * extent : (k + 1) * extent, part * extent : (part + 1) * extent] = out[
                    :, k * extent : (k + 1) * extent
                ]
        for k in range(modes):
            band = slice(k * extent, (k + 1) * extent)
            far[band, :] = jnp.dot(ybuf[band, :], col_table[...], preferred_element_type=F32)

    rows_then_cols(fr, frt)

    @pl.loop(0, n_chunks, unroll=4)
    def _(i):
        rb = pl.multiple_of(i * CHUNK, CHUNK)
        parts = []
        intensity = jnp.zeros((CHUNK, extent), F32)
        for k in range(modes):
            at = pl.ds(k * extent + rb, CHUNK)
            re, im = far[at, :extent], far[at, extent:]
            intensity += re * re + im * im
            parts.append((re, im))
        factor = amp[0, pl.ds(rb, CHUNK), :] * jnp.minimum(lax.rsqrt(intensity), 4.0)
        for k in range(modes):
            cols = slice(k * extent, (k + 1) * extent)
            xbuf[pl.ds(rb, CHUNK), cols] = (parts[k][0] * factor).astype(BF16)
            xbuf[pl.ds(extent + rb, CHUNK), cols] = (parts[k][1] * factor).astype(BF16)

    rows_then_cols(frt, fr)

    @pl.loop(0, n_chunks, unroll=4)
    def _(i):
        rb = pl.multiple_of(i * CHUNK, CHUNK)
        here = pl.ds(rb, CHUNK)
        wr, wi = win[0, here, :], win[1, here, :]
        obj_re = jnp.zeros((CHUNK, extent), F32)
        obj_im = jnp.zeros((CHUNK, extent), F32)
        for k in range(modes):
            at = pl.ds(k * extent + rb, CHUNK)
            dr = far[at, :extent] - psi[k, 0, here, :]
            di = far[at, extent:] - psi[k, 1, here, :]
            pr, pi = probe[k, 0, here, :], probe[k, 1, here, :]
            obj_re += pr * dr + pi * di
            obj_im += pr * di - pi * dr
            sums[2 * k, here, :] += wr * dr + wi * di
            sums[2 * k + 1, here, :] += wr * di - wi * dr
        blank = jnp.zeros((CHUNK, width - extent), F32)
        below = jnp.zeros((SUB, width), F32)
        for part, value in enumerate((obj_re, obj_im)):
            line = pltpu.roll(jnp.concatenate([value, blank], 1), lax.rem(c0, width), 1)
            line = pltpu.roll(jnp.concatenate([line, below], 0), low, 0)
            acc[part, pl.ds(pl.multiple_of(base + rb, SUB), tall), :] += line


def reduce_plan(n_gx, n_gy):
    x_bits, y_bits = n_gx.bit_length() - 1, n_gy.bit_length() - 1
    core, x, y = ("gy", 0, 1), ("gx", 0, 1), ("gy", 1, 1)
    z = ("gx", 1, min(2, x_bits - 1))
    rest = [("gx", b, 1) for b in range(3, x_bits)] + [("gy", b, 1) for b in range(2, y_bits)]
    return ([core, x, y, z] + rest, [core, y, x, z] + rest)


def fold_kernel(n_gx, n_gy, margin, acc, obj, probe, sums, out_obj, out_probe, *scratch):
    (from_left, from_right, send_up, send_down, from_up, from_down, part, inbox, sems) = scratch
    gx, gy = lax.axis_index("gx"), lax.axis_index("gy")
    rows, cols = obj.shape[1], obj.shape[2]
    planes, extent = sums.shape[0], sums.shape[1]
    modes = probe.shape[0]
    m = margin
    up = (lax.rem(gx + n_gx - 1, n_gx), gy)
    down = (lax.rem(gx + 1, n_gx), gy)
    left = (gx, lax.rem(gy + n_gy - 1, n_gy))
    right = (gx, lax.rem(gy + 1, n_gy))
    plan = reduce_plan(n_gx, n_gy)

    def members(axis, bit, count):
        size, step = 1 << count, 1 << bit
        coord = gx if axis == "gx" else gy
        mine = lax.rem(coord // step, size)
        peers = []
        for d in range(1, size):
            field = lax.rem(mine + d, size)
            other = coord + step * (field - mine)
            peers.append((field, (other, gy) if axis == "gx" else (gx, other)))
        return size, mine, peers

    greet([up, down, left, right] + [dev for g in plan[0] for _, dev in members(*g)[2]])

    slot = [0]
    pending = []

    def send(src, dst, device):
        copy = remote(src, dst, sems, slot[0], device)
        slot[0] += 1
        copy.start()
        pending.append(copy)
        return copy

    lcol, rcol = pl.ds(0, m), pl.ds(m + cols, m)
    bands = (pl.ds(0, m), pl.ds(m + rows, m))
    mid = pl.ds(m, rows)

    def strip(band):
        return (
            send(acc.at[:, band, lcol], from_right.at[:, band, :], left),
            send(acc.at[:, band, rcol], from_left.at[:, band, :], right),
        )

    lanes = len(plan)
    lane_w = extent // lanes
    state = [{"off": 0, "n": extent, "src": sums, "box": 0} for _ in range(lanes)]
    history = [[] for _ in range(lanes)]

    def reduce_start(step):
        started = []
        for lane in range(lanes):
            s = state[lane]
            size, mine, peers = members(*plan[lane][step])
            at = pl.ds(lane * lane_w, lane_w)
            split = s["n"] % (size * SUB) == 0
            n = s["n"] // size if split else s["n"]
            copies = []
            for field, device in peers:
                give = s["off"] + field * n if split else s["off"]
                src = s["src"].at[:, pl.ds(pl.multiple_of(give, SUB), n), at]
                box = inbox.at[:, pl.ds(pl.multiple_of(s["box"] + mine * n, SUB), n), at]
                copies.append(send(src, box, device))
            keep = s["off"] + mine * n if split else s["off"]
            history[lane].append((size, mine, peers, split))
            started.append((copies, keep, n, size, mine, s["box"]))
            s["box"] += size * n
        return started

    def reduce_end(step, started):
        for lane, (copies, keep, n, size, mine, box) in enumerate(started):
            s = state[lane]
            at = pl.ds(lane * lane_w, lane_w)
            own = s["src"][:, pl.ds(pl.multiple_of(keep, SUB), n), at]
            inbox[:, pl.ds(pl.multiple_of(box + mine * n, SUB), n), at] = own
            for copy in copies:
                copy.wait_recv()
            total = inbox[:, pl.ds(box, n), at]
            for j in range(1, size):
                total += inbox[:, pl.ds(box + j * n, n), at]
            part[step, :, pl.ds(pl.multiple_of(keep, SUB), n), at] = total
            s["off"], s["n"], s["src"] = keep, n, part.at[step]

    def fold_band(copies, band, buf):
        for copy in copies:
            copy.wait_recv()
        buf[:, :, :m] = acc[:, band, pl.ds(m, m)] + from_left[:, band, :]
        if cols > 2 * m:
            buf[:, :, m : cols - m] = acc[:, band, pl.ds(2 * m, cols - 2 * m)]
        buf[:, :, cols - m :] = acc[:, band, pl.ds(cols, m)] + from_right[:, band, :]

    piece = m // PIECES
    folded = []

    def vertical(ups, downs):
        for i in ups:
            at = pl.ds(i * piece, piece)
            folded.append(send(send_up.at[:, at, :], from_down.at[:, at, :], up))
        for i in downs:
            at = pl.ds(i * piece, piece)
            folded.append(send(send_down.at[:, at, :], from_up.at[:, at, :], down))

    def middle(i):
        folded.extend(strip(pl.ds(m + i * (rows // MIDS), rows // MIDS)))

    started = reduce_start(0)
    corner_up = strip(bands[0])
    reduce_end(0, started)
    started = reduce_start(1)
    corner_down = strip(bands[1])
    fold_band(corner_up, bands[0], send_up)
    vertical((0, 1), ())
    reduce_end(1, started)
    started = reduce_start(2)
    fold_band(corner_down, bands[1], send_down)
    vertical((2, 3), (0, 1))
    middle(0)
    reduce_end(2, started)
    steps = len(plan[0])
    started = reduce_start(3)
    vertical((4, 5), (2, 3))
    middle(1)
    reduce_end(3, started)
    for step in range(4, steps):
        started = reduce_start(step)
        reduce_end(step, started)

    for lane in range(lanes):
        s = state[lane]
        at = pl.ds(lane * lane_w, lane_w)
        keep = pl.ds(pl.multiple_of(s["off"], SUB), s["n"])
        weight = s["src"][planes - 1, keep, at] + 1e-05
        for k in range(2 * modes):
            out_probe[k, keep, at] = s["src"][k, keep, at] / weight

    def gather_start(level):
        started = []
        for lane in range(lanes):
            s = state[lane]
            size, mine, peers, split = history[lane][level]
            at = pl.ds(lane * lane_w, lane_w)
            if split:
                own = out_probe.at[:, pl.ds(pl.multiple_of(s["off"], SUB), s["n"]), at]
                started += [send(own, own, device) for _, device in peers]
                s["off"] = s["off"] - mine * s["n"]
                s["n"] *= size
        return started

    def gather_end(started):
        for copy in started:
            copy.wait_recv()

    started = gather_start(steps - 1)
    vertical((6, 7), (4, 5))
    middle(2)
    power = jnp.zeros((extent, extent), F32)
    for k in range(modes):
        for c in range(2):
            power += probe[k, c] * probe[k, c]
    scale = jnp.max(power, keepdims=True) + 1e-06
    for level in range(steps - 2, 0, -1):
        gather_end(started)
        started = gather_start(level)
        if level == 2:
            vertical((), (6, 7))
            middle(3)
    gather_end(started)
    started = gather_start(0)
    for copy in folded:
        copy.wait_recv()
    for c in range(2):
        step_sum = acc[c, pl.ds(m, rows), pl.ds(m, cols)]
        gap_r = [jnp.zeros((rows - 2 * m, cols), F32)] if rows > 2 * m else []
        gap_c = [jnp.zeros((rows, cols - 2 * m), F32)] if cols > 2 * m else []
        side = jnp.concatenate(
            [from_left[c, pl.ds(m, rows), :]] + gap_c + [from_right[c, pl.ds(m, rows), :]], 1
        )
        ends = jnp.concatenate([from_up[c]] + gap_r + [from_down[c]], 0)
        out_obj[c] = (step_sum + side + ends) / scale
    gather_end(started)
    for copy in pending:
        copy.wait_send()


def body(n_gx, n_gy, object_field, probe_field, amplitude, offsets):
    extent = probe_field.shape[-1]
    modes = probe_field.shape[0]
    margin = extent // 2
    rows, cols = object_field.shape[1:]
    positions = amplitude.shape[0]
    ext_shape = (2, rows + 2 * margin + SUB, cols + 2 * margin)
    ext = pl.pallas_call(
        functools.partial(halo_kernel, n_gx, n_gy, margin),
        out_shape=jax.ShapeDtypeStruct(ext_shape, F32),
        in_specs=[ANY],
        out_specs=VMEM,
        scratch_shapes=[pltpu.SemaphoreType.DMA((2, 2 + 6 * STRIPS)), pltpu.SemaphoreType.DMA((1,))],
        compiler_params=pltpu.CompilerParams(collective_id=0, has_side_effects=True),
        name="halo",
    )(object_field)

    planes = 2 * modes + 1
    acc, sums = pl.pallas_call(
        functools.partial(update_kernel, margin),
        grid=(positions,),
        out_shape=(
            jax.ShapeDtypeStruct(ext_shape, F32),
            jax.ShapeDtypeStruct((planes, extent, extent), F32),
        ),
        in_specs=[
            pl.BlockSpec(memory_space=pltpu.SMEM),
            VMEM,
            VMEM,
            pl.BlockSpec((1, extent, extent), lambda i: (i, 0, 0)),
            VMEM,
        ],
        out_specs=(VMEM, VMEM),
        scratch_shapes=[
            pltpu.VMEM((2, extent, extent), F32),
            pltpu.VMEM((modes, 2, extent, extent), F32),
            pltpu.VMEM((2 * extent, modes * extent), BF16),
            pltpu.VMEM((modes * extent, 2 * extent), BF16),
            pltpu.VMEM((modes * extent, 2 * extent), F32),
            pltpu.VMEM((2 * extent, 2 * extent), BF16),
            pltpu.VMEM((2 * extent, 2 * extent), BF16),
        ],
        name="update",
    )(offsets, ext, probe_field, amplitude[:, 0], dft_tables(extent))

    plan = reduce_plan(n_gx, n_gy)[0]
    steps = len(plan)
    peers = sum((1 << count) - 1 for _, _, count in plan)
    out_obj, out_probe = pl.pallas_call(
        functools.partial(fold_kernel, n_gx, n_gy, margin),
        out_shape=(
            jax.ShapeDtypeStruct(object_field.shape, F32),
            jax.ShapeDtypeStruct((2 * modes, extent, extent), F32),
        ),
        in_specs=[VMEM] * 4,
        out_specs=(VMEM, VMEM),
        scratch_shapes=[
            pltpu.VMEM((2, rows + 2 * margin, margin), F32),
            pltpu.VMEM((2, rows + 2 * margin, margin), F32),
            pltpu.VMEM((2, margin, cols), F32),
            pltpu.VMEM((2, margin, cols), F32),
            pltpu.VMEM((2, margin, cols), F32),
            pltpu.VMEM((2, margin, cols), F32),
            pltpu.VMEM((steps, planes, extent, extent), F32),
            pltpu.VMEM((planes, 3 * extent, extent), F32),
            pltpu.SemaphoreType.DMA((2, 4 + 2 * PIECES + 2 * MIDS + 4 * peers)),
        ],
        compiler_params=pltpu.CompilerParams(collective_id=1, has_side_effects=True),
        name="fold",
    )(acc, object_field, probe_field, sums)
    return object_field + out_obj, probe_field + out_probe.reshape(probe_field.shape)


def solution(mesh):
    in_specs = (P(None, "gx", "gy"), P(), P("gx", "gy", None, None), P("gx", "gy", None))
    out_specs = (P(None, "gx", "gy"), P())
    step = functools.partial(body, mesh.shape["gx"], mesh.shape["gy"])
    return jax.shard_map(step, mesh=mesh, in_specs=in_specs, out_specs=out_specs, check_vma=False)
```

```python
import functools
import math

import jax
import jax.numpy as jnp
import numpy as np
from jax import lax
from jax.experimental import pallas as pl
from jax.experimental.pallas import tpu as pltpu
from jax.sharding import PartitionSpec as P

MESH = pl.DeviceIdType.MESH
VMEM = pl.BlockSpec(memory_space=pltpu.VMEM)
ANY = pl.BlockSpec(memory_space=pl.ANY)
F32 = jnp.float32
BF16 = jnp.bfloat16
CHUNK = 32
SUB = 8
STRIPS = 4
PIECES = 8
MIDS = 4


def dft_tables(extent):
    indices = np.arange(extent)
    angles = (indices[:, None] * indices[None, :] % extent) * (2.0 * math.pi / extent)
    norm_factor = 1.0 / math.sqrt(extent)
    both = np.concatenate([np.cos(angles), np.sin(angles)], 1) * norm_factor
    return jnp.asarray(both.astype(np.float32).astype(jnp.bfloat16))


def remote(src, dst, sems, slot, device):
    return pltpu.make_async_remote_copy(
        src_ref=src,
        dst_ref=dst,
        send_sem=sems.at[0, slot],
        recv_sem=sems.at[1, slot],
        device_id=device,
        device_id_type=MESH,
    )


def greet(devices):
    barrier = pltpu.get_barrier_semaphore()
    for device in devices:
        pl.semaphore_signal(barrier, inc=1, device_id=device, device_id_type=MESH)
    pl.semaphore_wait(barrier, len(devices))


def halo_kernel(n_gx, n_gy, margin, obj, ext, sems, local_sem):
    gx, gy = lax.axis_index("gx"), lax.axis_index("gy")
    rows, cols = obj.shape[1], obj.shape[2]
    m = margin
    up = (lax.rem(gx + n_gx - 1, n_gx), gy)
    down = (lax.rem(gx + 1, n_gx), gy)
    left = (gx, lax.rem(gy + n_gy - 1, n_gy))
    right = (gx, lax.rem(gy + 1, n_gy))
    own = pltpu.make_async_copy(
        obj, ext.at[:, pl.ds(m, rows), pl.ds(m, cols)], local_sem.at[0]
    )
    own.start()
    greet((up, down, left, right))
    lcol, rcol = pl.ds(0, m), pl.ds(m + cols, m)
    mid_r, mid_c = pl.ds(m, rows), pl.ds(m, cols)
    piece = m // STRIPS
    slot = [0]

    def send(src, dst, device):
        copy = remote(src, dst, sems, slot[0], device)
        slot[0] += 1
        copy.start()
        return copy

    vertical = []
    for i in range(STRIPS):
        at = i * piece
        for src, dst, device in ((rows - m + at, at, down), (at, m + rows + at, up)):
            band = pl.ds(dst, piece)
            copy = send(obj.at[:, pl.ds(src, piece), :], ext.at[:, band, mid_c], device)
            vertical.append((copy, band))
    pending = [
        send(obj.at[:, :, pl.ds(cols - m, m)], ext.at[:, mid_r, lcol], right),
        send(obj.at[:, :, pl.ds(0, m)], ext.at[:, mid_r, rcol], left),
    ]
    for copy, band in vertical:
        copy.wait_recv()
        pending.append(send(ext.at[:, band, pl.ds(cols, m)], ext.at[:, band, lcol], right))
        pending.append(send(ext.at[:, band, pl.ds(m, m)], ext.at[:, band, rcol], left))
    for copy in pending:
        copy.wait_recv()
    for copy in pending:
        copy.wait_send()
    for copy, _ in vertical:
        copy.wait_send()
    own.wait()


def update_kernel(
    margin, offs, ext, probe, amp, table, acc, sums, win, psi, xbuf, ybuf, far, fr, frt
):
    p = pl.program_id(0)
    extent = probe.shape[-1]
    modes = probe.shape[0]
    width = ext.shape[2]
    r0 = offs[p, 0, 0] + margin
    c0 = offs[p, 0, 1] + margin
    back_shift = lax.rem(width - c0, width)
    low = lax.rem(r0, SUB)
    base = r0 - low
    tall = CHUNK + SUB
    row_shift = lax.rem(tall - low, tall)
    n_chunks = extent // CHUNK

    @pl.when(p == 0)
    def _():
        acc[...] = jnp.zeros_like(acc)
        sums[...] = jnp.zeros_like(sums)
        c, s = table[:, :extent], table[:, extent:]
        fr[:extent, :extent] = c
        fr[:extent, extent:] = s
        fr[extent:, :extent] = -s
        fr[extent:, extent:] = c
        frt[:extent, :extent] = c
        frt[:extent, extent:] = -s
        frt[extent:, :extent] = s
        frt[extent:, extent:] = c

    @pl.loop(0, n_chunks, unroll=8)
    def _(i):
        rb = pl.multiple_of(i * CHUNK, CHUNK)
        here = pl.ds(rb, CHUNK)
        w = []
        for part in range(2):
            line = ext[part, pl.ds(pl.multiple_of(base + rb, SUB), tall), :]
            line = pltpu.roll(line, row_shift, 0)[:CHUNK]
            w.append(pltpu.roll(line, back_shift, 1)[:, :extent])
            win[part, here, :] = w[part]
        sums[2 * modes, here, :] += w[0] * w[0] + w[1] * w[1]
        for k in range(modes):
            cols = slice(k * extent, (k + 1) * extent)
            pr, pi = probe[k, 0, here, :], probe[k, 1, here, :]
            psi_re = pr * w[0] - pi * w[1]
            psi_im = pr * w[1] + pi * w[0]
            psi[k, 0, here, :] = psi_re
            psi[k, 1, here, :] = psi_im
            xbuf[here, cols] = psi_re.astype(BF16)
            xbuf[pl.ds(extent + rb, CHUNK), cols] = psi_im.astype(BF16)

    def rows_then_cols(row_table, col_table):
        for part in range(2):
            table = row_table[part * extent : (part + 1) * extent, :]
            out = jnp.dot(table, xbuf[...], preferred_element_type=F32).astype(BF16)
            for k in range(modes):
                ybuf[k * extent : (k + 1) * extent, part * extent : (part + 1) * extent] = out[
                    :, k * extent : (k + 1) * extent
                ]
        for k in range(modes):
            band = slice(k * extent, (k + 1) * extent)
            far[band, :] = jnp.dot(ybuf[band, :], col_table[...], preferred_element_type=F32)

    rows_then_cols(fr, frt)

    @pl.loop(0, n_chunks, unroll=8)
    def _(i):
        rb = pl.multiple_of(i * CHUNK, CHUNK)
        parts = []
        intensity = jnp.zeros((CHUNK, extent), F32)
        for k in range(modes):
            at = pl.ds(k * extent + rb, CHUNK)
            re, im = far[at, :extent], far[at, extent:]
            intensity += re * re + im * im
            parts.append((re, im))
        factor = amp[0, pl.ds(rb, CHUNK), :] * jnp.minimum(lax.rsqrt(intensity), 4.0)
        for k in range(modes):
            cols = slice(k * extent, (k + 1) * extent)
            xbuf[pl.ds(rb, CHUNK), cols] = (parts[k][0] * factor).astype(BF16)
            xbuf[pl.ds(extent + rb, CHUNK), cols] = (parts[k][1] * factor).astype(BF16)

    rows_then_cols(frt, fr)

    @pl.loop(0, n_chunks, unroll=8)
    def _(i):
        rb = pl.multiple_of(i * CHUNK, CHUNK)
        here = pl.ds(rb, CHUNK)
        wr, wi = win[0, here, :], win[1, here, :]
        obj_re = jnp.zeros((CHUNK, extent), F32)
        obj_im = jnp.zeros((CHUNK, extent), F32)
        for k in range(modes):
            at = pl.ds(k * extent + rb, CHUNK)
            dr = far[at, :extent] - psi[k, 0, here, :]
            di = far[at, extent:] - psi[k, 1, here, :]
            pr, pi = probe[k, 0, here, :], probe[k, 1, here, :]
            obj_re += pr * dr + pi * di
            obj_im += pr * di - pi * dr
            sums[2 * k, here, :] += wr * dr + wi * di
            sums[2 * k + 1, here, :] += wr * di - wi * dr
        blank = jnp.zeros((CHUNK, width - extent), F32)
        below = jnp.zeros((SUB, width), F32)
        for part, value in enumerate((obj_re, obj_im)):
            line = pltpu.roll(jnp.concatenate([value, blank], 1), lax.rem(c0, width), 1)
            line = pltpu.roll(jnp.concatenate([line, below], 0), low, 0)
            acc[part, pl.ds(pl.multiple_of(base + rb, SUB), tall), :] += line


def reduce_plan(n_gx, n_gy):
    x_bits, y_bits = n_gx.bit_length() - 1, n_gy.bit_length() - 1
    core, x, y = ("gy", 0, 1), ("gx", 0, 1), ("gy", 1, 1)
    z = ("gx", 1, min(2, x_bits - 1))
    rest = [("gx", b, 1) for b in range(3, x_bits)] + [("gy", b, 1) for b in range(2, y_bits)]
    return ([core, x, y, z] + rest, [core, y, x, z] + rest)


def fold_kernel(n_gx, n_gy, margin, acc, obj, probe, sums, out_obj, out_probe, *scratch):
    (from_left, from_right, send_up, send_down, from_up, from_down, part, inbox, sems) = scratch
    gx, gy = lax.axis_index("gx"), lax.axis_index("gy")
    rows, cols = obj.shape[1], obj.shape[2]
    planes, extent = sums.shape[0], sums.shape[1]
    modes = probe.shape[0]
    m = margin
    up = (lax.rem(gx + n_gx - 1, n_gx), gy)
    down = (lax.rem(gx + 1, n_gx), gy)
    left = (gx, lax.rem(gy + n_gy - 1, n_gy))
    right = (gx, lax.rem(gy + 1, n_gy))
    plan = reduce_plan(n_gx, n_gy)

    def members(axis, bit, count):
        size, step = 1 << count, 1 << bit
        coord = gx if axis == "gx" else gy
        mine = lax.rem(coord // step, size)
        peers = []
        for d in range(1, size):
            field = lax.rem(mine + d, size)
            other = coord + step * (field - mine)
            peers.append((field, (other, gy) if axis == "gx" else (gx, other)))
        return size, mine, peers

    greet([up, down, left, right] + [dev for g in plan[0] for _, dev in members(*g)[2]])

    slot = [0]
    pending = []

    def send(src, dst, device):
        copy = remote(src, dst, sems, slot[0], device)
        slot[0] += 1
        copy.start()
        pending.append(copy)
        return copy

    lcol, rcol = pl.ds(0, m), pl.ds(m + cols, m)
    bands = (pl.ds(0, m), pl.ds(m + rows, m))
    mid = pl.ds(m, rows)

    def strip(band):
        return (
            send(acc.at[:, band, lcol], from_right.at[:, band, :], left),
            send(acc.at[:, band, rcol], from_left.at[:, band, :], right),
        )

    lanes = len(plan)
    lane_w = extent // lanes
    state = [{"off": 0, "n": extent, "src": sums, "box": 0} for _ in range(lanes)]
    history = [[] for _ in range(lanes)]

    def reduce_start(step):
        started = []
        for lane in range(lanes):
            s = state[lane]
            size, mine, peers = members(*plan[lane][step])
            at = pl.ds(lane * lane_w, lane_w)
            split = s["n"] % (size * SUB) == 0
            n = s["n"] // size if split else s["n"]
            copies = []
            for field, device in peers:
                give = s["off"] + field * n if split else s["off"]
                src = s["src"].at[:, pl.ds(pl.multiple_of(give, SUB), n), at]
                box = inbox.at[:, pl.ds(pl.multiple_of(s["box"] + mine * n, SUB), n), at]
                copies.append(send(src, box, device))
            keep = s["off"] + mine * n if split else s["off"]
            history[lane].append((size, mine, peers, split))
            started.append((copies, keep, n, size, mine, s["box"]))
            s["box"] += size * n
        return started

    def reduce_end(step, started):
        for lane, (copies, keep, n, size, mine, box) in enumerate(started):
            s = state[lane]
            at = pl.ds(lane * lane_w, lane_w)
            own = s["src"][:, pl.ds(pl.multiple_of(keep, SUB), n), at]
            inbox[:, pl.ds(pl.multiple_of(box + mine * n, SUB), n), at] = own
            for copy in copies:
                copy.wait_recv()
            total = inbox[:, pl.ds(box, n), at]
            for j in range(1, size):
                total += inbox[:, pl.ds(box + j * n, n), at]
            part[step, :, pl.ds(pl.multiple_of(keep, SUB), n), at] = total
            s["off"], s["n"], s["src"] = keep, n, part.at[step]

    def fold_band(copies, band, buf):
        for copy in copies:
            copy.wait_recv()
        buf[:, :, :m] = acc[:, band, pl.ds(m, m)] + from_left[:, band, :]
        if cols > 2 * m:
            buf[:, :, m : cols - m] = acc[:, band, pl.ds(2 * m, cols - 2 * m)]
        buf[:, :, cols - m :] = acc[:, band, pl.ds(cols, m)] + from_right[:, band, :]

    piece = m // PIECES
    folded = []

    def vertical(ups, downs):
        for i in ups:
            at = pl.ds(i * piece, piece)
            folded.append(send(send_up.at[:, at, :], from_down.at[:, at, :], up))
        for i in downs:
            at = pl.ds(i * piece, piece)
            folded.append(send(send_down.at[:, at, :], from_up.at[:, at, :], down))

    def middle(i):
        folded.extend(strip(pl.ds(m + i * (rows // MIDS), rows // MIDS)))

    started = reduce_start(0)
    corner_up = strip(bands[0])
    reduce_end(0, started)
    started = reduce_start(1)
    corner_down = strip(bands[1])
    fold_band(corner_up, bands[0], send_up)
    vertical((0, 1), ())
    reduce_end(1, started)
    started = reduce_start(2)
    fold_band(corner_down, bands[1], send_down)
    vertical((2, 3), (0, 1))
    middle(0)
    reduce_end(2, started)
    steps = len(plan[0])
    started = reduce_start(3)
    vertical((4, 5), (2, 3))
    middle(1)
    reduce_end(3, started)
    for step in range(4, steps):
        started = reduce_start(step)
        reduce_end(step, started)

    for lane in range(lanes):
        s = state[lane]
        at = pl.ds(lane * lane_w, lane_w)
        keep = pl.ds(pl.multiple_of(s["off"], SUB), s["n"])
        weight = s["src"][planes - 1, keep, at] + 1e-05
        for k in range(2 * modes):
            out_probe[k, keep, at] = s["src"][k, keep, at] / weight

    def gather_start(level):
        started = []
        for lane in range(lanes):
            s = state[lane]
            size, mine, peers, split = history[lane][level]
            at = pl.ds(lane * lane_w, lane_w)
            if split:
                own = out_probe.at[:, pl.ds(pl.multiple_of(s["off"], SUB), s["n"]), at]
                started += [send(own, own, device) for _, device in peers]
                s["off"] = s["off"] - mine * s["n"]
                s["n"] *= size
        return started

    def gather_end(started):
        for copy in started:
            copy.wait_recv()

    started = gather_start(steps - 1)
    vertical((6, 7), (4, 5))
    middle(2)
    power = jnp.zeros((extent, extent), F32)
    for k in range(modes):
        for c in range(2):
            power += probe[k, c] * probe[k, c]
    scale = jnp.max(power, keepdims=True) + 1e-06
    for level in range(steps - 2, 0, -1):
        gather_end(started)
        started = gather_start(level)
        if level == 2:
            vertical((), (6, 7))
            middle(3)
    gather_end(started)
    started = gather_start(0)
    for copy in folded:
        copy.wait_recv()
    for c in range(2):
        step_sum = acc[c, pl.ds(m, rows), pl.ds(m, cols)]
        gap_r = [jnp.zeros((rows - 2 * m, cols), F32)] if rows > 2 * m else []
        gap_c = [jnp.zeros((rows, cols - 2 * m), F32)] if cols > 2 * m else []
        side = jnp.concatenate(
            [from_left[c, pl.ds(m, rows), :]] + gap_c + [from_right[c, pl.ds(m, rows), :]], 1
        )
        ends = jnp.concatenate([from_up[c]] + gap_r + [from_down[c]], 0)
        out_obj[c] = (step_sum + side + ends) / scale
    gather_end(started)
    for copy in pending:
        copy.wait_send()


def body(n_gx, n_gy, object_field, probe_field, amplitude, offsets):
    extent = probe_field.shape[-1]
    modes = probe_field.shape[0]
    margin = extent // 2
    rows, cols = object_field.shape[1:]
    positions = amplitude.shape[0]
    ext_shape = (2, rows + 2 * margin + SUB, cols + 2 * margin)
    ext = pl.pallas_call(
        functools.partial(halo_kernel, n_gx, n_gy, margin),
        out_shape=jax.ShapeDtypeStruct(ext_shape, F32),
        in_specs=[ANY],
        out_specs=VMEM,
        scratch_shapes=[pltpu.SemaphoreType.DMA((2, 2 + 6 * STRIPS)), pltpu.SemaphoreType.DMA((1,))],
        compiler_params=pltpu.CompilerParams(collective_id=0, has_side_effects=True),
        name="halo",
    )(object_field)

    planes = 2 * modes + 1
    acc, sums = pl.pallas_call(
        functools.partial(update_kernel, margin),
        grid=(positions,),
        out_shape=(
            jax.ShapeDtypeStruct(ext_shape, F32),
            jax.ShapeDtypeStruct((planes, extent, extent), F32),
        ),
        in_specs=[
            pl.BlockSpec(memory_space=pltpu.SMEM),
            VMEM,
            VMEM,
            pl.BlockSpec((1, extent, extent), lambda i: (i, 0, 0)),
            VMEM,
        ],
        out_specs=(VMEM, VMEM),
        scratch_shapes=[
            pltpu.VMEM((2, extent, extent), F32),
            pltpu.VMEM((modes, 2, extent, extent), F32),
            pltpu.VMEM((2 * extent, modes * extent), BF16),
            pltpu.VMEM((modes * extent, 2 * extent), BF16),
            pltpu.VMEM((modes * extent, 2 * extent), F32),
            pltpu.VMEM((2 * extent, 2 * extent), BF16),
            pltpu.VMEM((2 * extent, 2 * extent), BF16),
        ],
        name="update",
    )(offsets, ext, probe_field, amplitude[:, 0], dft_tables(extent))

    plan = reduce_plan(n_gx, n_gy)[0]
    steps = len(plan)
    peers = sum((1 << count) - 1 for _, _, count in plan)
    out_obj, out_probe = pl.pallas_call(
        functools.partial(fold_kernel, n_gx, n_gy, margin),
        out_shape=(
            jax.ShapeDtypeStruct(object_field.shape, F32),
            jax.ShapeDtypeStruct((2 * modes, extent, extent), F32),
        ),
        in_specs=[VMEM] * 4,
        out_specs=(VMEM, VMEM),
        scratch_shapes=[
            pltpu.VMEM((2, rows + 2 * margin, margin), F32),
            pltpu.VMEM((2, rows + 2 * margin, margin), F32),
            pltpu.VMEM((2, margin, cols), F32),
            pltpu.VMEM((2, margin, cols), F32),
            pltpu.VMEM((2, margin, cols), F32),
            pltpu.VMEM((2, margin, cols), F32),
            pltpu.VMEM((steps, planes, extent, extent), F32),
            pltpu.VMEM((planes, 3 * extent, extent), F32),
            pltpu.SemaphoreType.DMA((2, 4 + 2 * PIECES + 2 * MIDS + 4 * peers)),
        ],
        compiler_params=pltpu.CompilerParams(collective_id=1, has_side_effects=True),
        name="fold",
    )(acc, object_field, probe_field, sums)
    return object_field + out_obj, probe_field + out_probe.reshape(probe_field.shape)


def solution(mesh):
    in_specs = (P(None, "gx", "gy"), P(), P("gx", "gy", None, None), P("gx", "gy", None))
    out_specs = (P(None, "gx", "gy"), P())
    step = functools.partial(body, mesh.shape["gx"], mesh.shape["gy"])
    return jax.shard_map(step, mesh=mesh, in_specs=in_specs, out_specs=out_specs, check_vma=False)
```
